32 devices in a mesh: grp: 4 (over z), dev: 8 (over y, x, core).
Axes of the slice: x: 2, y: 2, z: 4, core: 2. Of those that a mesh axis runs over, the one named last changes fastest.
Arguments:
- fraction: float32 [64, 256, 1024], P('grp', 'dev'), may hold values from 0 to 1
- courant: float32 [64, 256, 1024], P('grp', 'dev'), may hold values from -0.45 to 0.45
- divergence: float32 [64, 256, 1024], P('grp', 'dev'), may hold values from -40 to 40
- densities: float32 [2], replicated, may hold values from 0.8 to 2.2
- band_tiles: int32 [4, 8, 128], P('grp', 'dev'), may hold values from -1 to 127, as said below
Outputs:
- new_fraction: float32 [64, 256, 1024], P('grp', 'dev')
- pressure: float32 [64, 256, 1024], P('grp', 'dev')
- residual: float32 [64, 256, 1024], P('grp', 'dev')
The draws below stay inside these ranges and needn't reach their ends.
Inputs may be any that keep to these rules, and one draw needn't show every extreme that they name: `band_tiles`: each list holds distinct tile numbers first and -1 after them. In every group along dev the lists name 32 tiles a device on average, exactly, and one device of every group lists all 128 of its tiles.
All inputs are finite; a program needn't handle non-finite values.
Results may differ from the reference program's by a relative error of at most 0.012.
Values sent between devices are 32-bit elements; how exact they have to be, the bound alone decides.
A program may use at most 192 MiB of HBM per device.

```python
import math
import jax
import jax.numpy as jnp
from jax import lax

TILE = 16
TX_DEV = 2
TY = 64
ITERS = 2
TPD = 128
HCAP = 32
NY = 1024
NZ = 64
NX = 256
N_GRP = 4
N_DEV = 8


def group_counts(key):
    key_order, key_moves = jax.random.split(key)
    order = jax.random.permutation(key_order, N_DEV)
    rank_of = jnp.argsort(order).astype(jnp.int32)
    other_rank = rank_of - 1
    removal_total = 3 * HCAP
    taken = jnp.where((other_rank >= 0) & (other_rank < removal_total), (removal_total - 1 - other_rank) // (N_DEV - 1) + 1, 0)
    counts = jnp.where(rank_of == 0, TPD, HCAP - taken).astype(jnp.int32)
    for turn in range(8):
        key_moves, key_pick = jax.random.split(key_moves)
        chosen = jax.random.randint(key_pick, (2,), 0, N_DEV)
        donor = chosen[0]
        taker = chosen[1]
        allowed = (donor != taker) & (rank_of[donor] != 0) & (rank_of[taker] != 0) & (counts[donor] > 0) & (counts[taker] < TPD - 1)
        moving = allowed.astype(jnp.int32)
        counts = counts.at[donor].add(-moving).at[taker].add(moving)
    return counts


def draw_band_tiles(key, part):
    group_keys = jax.random.split(jax.random.fold_in(key, 11), N_GRP)
    counts = jax.vmap(group_counts)(group_keys)
    device_keys = jax.random.split(jax.random.fold_in(key, 23), N_GRP * N_DEV)
    orders = jax.vmap(lambda single: jax.random.permutation(single, TPD))(device_keys).reshape(N_GRP, N_DEV, TPD).astype(jnp.int32)
    positions = jnp.arange(TPD, dtype=jnp.int32)
    return jnp.where(positions[None, None, :] < counts[:, :, None], orders, -1).astype(jnp.int32)


def draw_divergence(key, part):
    first_pos = (jnp.arange(NZ, dtype=jnp.float32) + 0.5) / NZ
    second_pos = (jnp.arange(NX, dtype=jnp.float32) + 0.5) / NX
    rising = jnp.exp(0.5 * math.log(3.0) * (first_pos[:, None, None] + second_pos[None, :, None]))
    rough = jnp.clip(jax.random.normal(key, (NZ, NX, NY), jnp.float32), -6.0, 6.0)
    values = 2.0 * rising * rough
    return values.astype(jnp.float32)


def block_levels(own_key, shape, cuts, least, high):
    def one(axis_at, shards_of):
        heights = jax.random.uniform(jax.random.fold_in(jax.random.fold_in(own_key, 6), axis_at), (shards_of,), jnp.float32, least / len(cuts), high / len(cuts))
        return jnp.repeat(jnp.exp(heights), shape[axis_at] // shards_of).reshape((-1,) + (1,) * (len(shape) - axis_at - 1))

    factor_of = one(*cuts[0])
    for cut in cuts[1:]:
        factor_of = factor_of * one(*cut)
    return factor_of


def setup_inputs(seed: int = 0) -> dict:
    key_of = jax.random.split(jax.random.key(seed), 6)
    return {
        "fraction": jnp.clip(1.0 * jax.random.uniform(key_of[0], (NZ, NX, NY), jnp.float32) ** block_levels(key_of[0], (NZ, NX, NY), ((0, 4), (1, 8)), -0.2, 0.2), 0.0, 1.0),
        "courant": jnp.clip(jax.random.uniform(key_of[1], (NZ, NX, NY), jnp.float32, -0.45, 0.45) * block_levels(key_of[1], (NZ, NX, NY), ((0, 4), (1, 8)), -0.4, 0.0), -0.45, 0.45),
        "divergence": draw_divergence(jax.random.fold_in(key_of[5], 71), 0),
        "densities": jnp.clip(jnp.exp(jax.random.uniform(key_of[3], (2,), jnp.float32, math.log(0.8), math.log(2.2))), 0.8, 2.2),
        "band_tiles": draw_band_tiles(jax.random.fold_in(key_of[5], 71), 0),
    }


def advect(extended, speeds):
    forward = extended[..., 1:] - extended[..., :-1]
    ahead_diff = forward[..., 1:]
    behind = forward[..., :-1]
    slopes = 0.5 * (jnp.sign(ahead_diff) + jnp.sign(behind)) * jnp.minimum(jnp.abs(ahead_diff), jnp.abs(behind))
    face_span = speeds.shape[-1] - 1
    left_cell = extended[..., 1:face_span + 2]
    right_cell = extended[..., 2:face_span + 3]
    slope_left = slopes[..., 0:face_span + 1]
    slope_right = slopes[..., 1:face_span + 2]
    fluxes = jnp.where(speeds > 0, speeds * (left_cell + 0.5 * (1.0 - speeds) * slope_left), speeds * (right_cell - 0.5 * (1.0 + speeds) * slope_right))
    return jnp.clip(extended[..., 2:face_span + 2] - (fluxes[..., 1:] - fluxes[..., :-1]), 0.0, 1.0)


def coefficients(density):
    beta_first = 2.0 / (density[:-1, 1:-1, 1:-1] + density[1:, 1:-1, 1:-1])
    beta_second = 2.0 / (density[1:-1, :-1, 1:-1] + density[1:-1, 1:, 1:-1])
    beta_third = 2.0 / (density[1:-1, 1:-1, :-1] + density[1:-1, 1:-1, 1:])
    return beta_first, beta_second, beta_third


def apply_operator(field, padded, betas):
    beta_first, beta_second, beta_third = betas
    result = beta_first[1:] * (field - padded[2:, 1:-1, 1:-1]) + beta_first[:-1] * (field - padded[:-2, 1:-1, 1:-1])
    result = result + beta_second[:, 1:] * (field - padded[1:-1, 2:, 1:-1]) + beta_second[:, :-1] * (field - padded[1:-1, :-2, 1:-1])
    result = result + beta_third[:, :, 1:] * (field - padded[1:-1, 1:-1, 2:]) + beta_third[:, :, :-1] * (field - padded[1:-1, 1:-1, :-2])
    return result


def reference(fraction, courant, divergence, densities, band_tiles):
    grid_shape = fraction.shape
    y_index = lax.broadcasted_iota(jnp.int32, grid_shape, 2)
    speed_field = jnp.where(y_index > 0, courant, jnp.zeros_like(courant))
    speeds = jnp.concatenate([speed_field, jnp.zeros((grid_shape[0], grid_shape[1], 1), courant.dtype)], axis=2)
    extended = jnp.pad(fraction, ((0, 0), (0, 0), (2, 2)))
    advected = advect(extended, speeds)
    tile_ids = jnp.arange(TPD, dtype=jnp.int32)
    present = jnp.any(band_tiles[..., :, None] == tile_ids, axis=-2)
    in_band = jnp.broadcast_to(present.reshape(N_GRP, 1, N_DEV, TX_DEV, 1, TY, 1), (N_GRP, TILE, N_DEV, TX_DEV, TILE, TY, TILE)).reshape(grid_shape)
    new_fraction = jnp.where(in_band, advected, fraction)

    outer = jnp.pad(fraction, 1)
    density = outer * densities[0] + (1.0 - outer) * densities[1]
    betas = coefficients(density)
    pressure = jnp.zeros_like(divergence)
    residual = divergence
    direction = divergence
    norm_now = jnp.sum(residual * residual)
    for iteration in range(ITERS):
        image_vec = apply_operator(direction, jnp.pad(direction, 1), betas)
        step_length = norm_now / jnp.sum(direction * image_vec)
        pressure = pressure + step_length * direction
        residual = residual - step_length * image_vec
        norm_next = jnp.sum(residual * residual)
        direction = residual + (norm_next / norm_now) * direction
        norm_now = norm_next
    return new_fraction, pressure, residual
```

```python
import functools

import jax
import jax.numpy as jnp
from jax import lax
from jax.experimental import pallas as pl
from jax.experimental.pallas import tpu as pltpu
from jax.sharding import PartitionSpec as P

TILE = 16
SUB = 8
LANES = 128
MESH = pl.DeviceIdType.MESH


def fold(value):
    total = value[:, 0:LANES]
    for start in range(LANES, value.shape[1], LANES):
        total = total + value[:, start : start + LANES]
    return total


def kernel(
    sizes,
    frac_in,
    cour_in,
    div_in,
    dens,
    band,
    frac_out,
    pres_out,
    res_out,
    frac,
    cour,
    field,
    image,
    second,
    beta0,
    beta1,
    beta2,
    beta_last,
    mask,
    row_send,
    row_recv,
    sum_grp,
    sum_dev,
    load_sem,
    plane_send_sem,
    plane_recv_sem,
    row_send_sem,
    row_recv_sem,
    grp_send_sem,
    grp_recv_sem,
    dev_send_sem,
    dev_recv_sem,
):
    groups, devs = sizes
    depth, rows, width = frac_in.shape
    blocks = rows // SUB
    g = lax.axis_index("grp")
    d = lax.axis_index("dev")
    inner = pl.ds(SUB, rows)

    loads = []
    for slot, (source, target) in enumerate(
        (
            (frac_in, frac.at[pl.ds(1, depth), inner]),
            (div_in, field.at[pl.ds(1, depth), inner]),
            (cour_in, cour),
        )
    ):
        copy = pltpu.make_async_copy(source, target, load_sem.at[slot])
        copy.start()
        loads.append(copy)

    barrier = pltpu.get_barrier_semaphore()
    for step in range(1, groups):
        pl.semaphore_signal(
            barrier, inc=1, device_id={"grp": lax.rem(g + step, groups)}, device_id_type=MESH
        )
    for step in range(1, devs):
        pl.semaphore_signal(
            barrier, inc=1, device_id={"dev": lax.rem(d + step, devs)}, device_id_type=MESH
        )

    padded = (frac, field, image)
    edges = ((g > 0, g == 0), (g < groups - 1, g == groups - 1))
    row_edges = ((d > 0, d == 0), (d < devs - 1, d == devs - 1))

    for side in range(2):
        plane = 0 if side == 0 else depth + 1

        @pl.when(edges[side][1])
        def _():
            for target in padded:
                target[plane, inner, :] = jnp.zeros((rows, width), jnp.float32)

        @pl.when(row_edges[side][1])
        def _():
            for which in range(3):
                row_recv[which, side] = jnp.zeros((depth, width), jnp.float32)

    across = rows // TILE
    along = width // TILE
    ids = (
        lax.broadcasted_iota(jnp.int32, (SUB, width), 1) // TILE
        + lax.broadcasted_iota(jnp.int32, (SUB, width), 0) * along
    )

    def listed(entry, seen):
        return jnp.where(ids == band[entry], 1.0, seen)

    mask[...] = lax.fori_loop(
        0, across * along, listed, jnp.zeros((SUB, width), jnp.float32)
    )

    pl.semaphore_wait(barrier, groups + devs - 2)

    def plane_copy(which, source, side):
        target = padded[which]
        plane = depth + 1 if side == 0 else 0
        other = lax.rem(g + (groups - 1 if side == 0 else 1), groups)
        return pltpu.make_async_remote_copy(
            src_ref=source,
            dst_ref=target.at[plane, inner],
            send_sem=plane_send_sem.at[which, side],
            recv_sem=plane_recv_sem.at[which, 1 - side],
            device_id={"grp": other},
            device_id_type=MESH,
        )

    def row_copy(which, side):
        other = lax.rem(d + (devs - 1 if side == 0 else 1), devs)
        return pltpu.make_async_remote_copy(
            src_ref=row_send.at[which, side],
            dst_ref=row_recv.at[which, 1 - side],
            send_sem=row_send_sem.at[which, side],
            recv_sem=row_recv_sem.at[which, 1 - side],
            device_id={"dev": other},
            device_id_type=MESH,
        )

    def plane_source(which, side):
        plane = 0 if side == 0 else depth - 1
        if which == 2:
            return image.at[plane + 1, inner]
        return (frac_in, div_in)[which].at[plane]

    def send_planes(which):
        for side in range(2):

            @pl.when(edges[side][0])
            def _():
                plane_copy(which, plane_source(which, side), side).start()

    def send_rows(which):
        source = padded[which]

        def pack(i, carry):
            row_send[which, 0, pl.ds(i, 1), :] = source[i + 1, pl.ds(SUB, 1), :]
            row_send[which, 1, pl.ds(i, 1), :] = source[i + 1, pl.ds(SUB + rows - 1, 1), :]
            return carry

        lax.fori_loop(0, depth, pack, 0)
        for side in range(2):

            @pl.when(row_edges[side][0])
            def _():
                row_copy(which, side).start()

    def receive(which):
        for side in range(2):

            @pl.when(row_edges[side][0])
            def _():
                row_copy(which, side).wait_send()
                row_copy(which, 1 - side).wait_recv()

        target = padded[which]

        def unpack(i, carry):
            target[i + 1, pl.ds(SUB - 1, 1), :] = row_recv[which, 0, pl.ds(i, 1), :]
            target[i + 1, pl.ds(SUB + rows, 1), :] = row_recv[which, 1, pl.ds(i, 1), :]
            return carry

        lax.fori_loop(0, depth, unpack, 0)
        for side in range(2):

            @pl.when(edges[side][0])
            def _():
                plane_copy(which, plane_source(which, side), side).wait_send()
                plane_copy(which, plane_source(which, 1 - side), 1 - side).wait_recv()

    send_planes(0)
    send_planes(1)
    loads[0].wait()
    send_rows(0)
    loads[1].wait()
    send_rows(1)

    half0 = 0.5 * dens[0]
    half1 = 0.5 * dens[1]

    def half_density(value):
        return value * half0 + (1.0 - value) * half1

    lane = lax.broadcasted_iota(jnp.int32, (SUB, width), 1)
    first_lane = lane == 0
    last_lane = lane == width - 1
    tail = pl.ds(width - LANES, LANES)

    def chunk(block, offset=0):
        return pl.ds(SUB + block * SUB + offset, SUB)

    def local_betas(i, carry):
        for block in range(blocks):
            own = half_density(frac[i + 1, chunk(block), :])
            below = jnp.where(first_lane, half1, pltpu.roll(own, 1, 1))
            here = pl.ds(block * SUB, SUB)
            beta2[i, here, :] = 1.0 / (own + below)
            beta_last[i, here, :] = 1.0 / (own[:, width - LANES :] + half1)
        return carry

    lax.fori_loop(0, depth, local_betas, 0)

    def first_faces(i):
        for block in range(blocks):
            own = half_density(frac[i + 1, chunk(block), :])
            before = half_density(frac[i, chunk(block), :])
            beta0[i, pl.ds(block * SUB, SUB), :] = 1.0 / (own + before)

    def first_betas(i, carry):
        first_faces(i)
        return carry

    lax.fori_loop(1, depth, first_betas, 0)

    receive(0)
    first_faces(0)
    first_faces(depth)

    def second_betas(i, carry):
        for block in range(blocks):
            own = half_density(frac[i + 1, chunk(block), :])
            before = half_density(frac[i + 1, chunk(block, -1), :])
            beta1[i, pl.ds(block * SUB, SUB), :] = 1.0 / (own + before)
        own = half_density(frac[i + 1, pl.ds(SUB + rows, 1), :])
        before = half_density(frac[i + 1, pl.ds(SUB + rows - 1, 1), :])
        beta1[i, pl.ds(rows, 1), :] = 1.0 / (own + before)
        return carry

    lax.fori_loop(0, depth, second_betas, 0)

    receive(1)

    def operator(source, i, block):
        here = pl.ds(block * SUB, SUB)
        own = source[i + 1, chunk(block), :]
        result = beta0[i + 1, here, :] * (own - source[i + 2, chunk(block), :])
        result = result + beta0[i, here, :] * (own - source[i, chunk(block), :])
        result = result + beta1[i, pl.ds(block * SUB + 1, SUB), :] * (
            own - source[i + 1, chunk(block, 1), :]
        )
        result = result + beta1[i, here, :] * (own - source[i + 1, chunk(block, -1), :])
        below = jnp.where(first_lane, 0.0, pltpu.roll(own, 1, 1))
        low = beta2[i, here, :] * (own - below)
        end = beta_last[i, here, :] * own[:, width - LANES :]
        end = jnp.concatenate([low[:, : width - LANES], end], axis=1)
        high = jnp.where(last_lane, -end, pltpu.roll(low, width - 1, 1))
        return own, result + (low - high)

    def first_image(i, carry):
        norm, cross = carry
        for block in range(blocks):
            own, result = operator(field, i, block)
            image[i + 1, chunk(block), :] = result
            norm = norm + fold(own * own)
            cross = cross + fold(own * result)
        return norm, cross

    nothing = jnp.zeros((SUB, LANES), jnp.float32)
    norm, cross = lax.fori_loop(0, depth, first_image, (nothing, nothing))

    unit = lax.broadcasted_iota(jnp.int32, (1, LANES), 1)

    def message(parts):
        value = jnp.zeros((1, LANES), jnp.float32)
        for place, part in enumerate(parts):
            value = jnp.where(unit == place, jnp.sum(part), value)
        return value

    def stage(phase, axis, buffer, send_sem, recv_sem, index, count):
        def copy(step):
            return pltpu.make_async_remote_copy(
                src_ref=buffer.at[phase, index],
                dst_ref=buffer.at[phase, index],
                send_sem=send_sem.at[phase, step],
                recv_sem=recv_sem.at[phase, step],
                device_id={axis: lax.rem(index + step, count)},
                device_id_type=MESH,
            )

        def start(value):
            buffer[phase, pl.ds(index, 1)] = value.reshape(1, 1, LANES)
            for step in range(1, count):
                copy(step).start()

        def finish():
            for step in range(1, count):
                copy(step).wait()
            total = buffer[phase, 0]
            for other in range(1, count):
                total = total + buffer[phase, other]
            return total

        return start, finish

    def across_grp(phase):
        return stage(phase, "grp", sum_grp, grp_send_sem, grp_recv_sem, g, groups)

    def across_dev(phase):
        return stage(phase, "dev", sum_dev, dev_send_sem, dev_recv_sem, d, devs)

    def pick(total, place):
        return jnp.sum(jnp.where(unit == place, total, 0.0), axis=1, keepdims=True)

    send_planes(2)
    start_grp, finish_grp = across_grp(0)
    start_grp(message((norm, cross)))
    send_rows(2)

    loads[2].wait()

    def advect(i, carry):
        for block in range(blocks):
            own = frac[i + 1, chunk(block), :]
            speed = jnp.where(first_lane, 0.0, cour[i, pl.ds(block * SUB, SUB), :])
            left = jnp.where(first_lane, 0.0, pltpu.roll(own, 1, 1))
            behind = own - left
            ahead = jnp.where(last_lane, -own, pltpu.roll(behind, width - 1, 1))
            slope = jnp.maximum(0.0, jnp.minimum(ahead, behind)) + jnp.minimum(
                0.0, jnp.maximum(ahead, behind)
            )
            forward = speed > 0
            upwind = jnp.where(forward, left, own)
            tilt = jnp.where(forward, pltpu.roll(slope, 1, 1), -slope)
            flux = speed * (upwind + 0.5 * (1.0 - jnp.abs(speed)) * tilt)
            moved = jnp.clip(own - (pltpu.roll(flux, width - 1, 1) - flux), 0.0, 1.0)
            flag = mask[pl.ds(block * SUB // TILE, 1), :]
            frac_out[i, pl.ds(block * SUB, SUB), :] = jnp.where(flag > 0.5, moved, own)
        return carry

    half_way = depth // 2
    lax.fori_loop(0, half_way, advect, 0)
    start_dev, finish_dev = across_dev(0)
    start_dev(finish_grp())
    lax.fori_loop(half_way, depth, advect, 0)

    receive(2)

    def second_image(i, carry):
        for block in range(blocks):
            own, result = operator(image, i, block)
            second[i, pl.ds(block * SUB, SUB), :] = result
        return carry

    lax.fori_loop(0, depth, second_image, 0)

    total = finish_dev()
    norm0 = pick(total, 0)
    cross0 = pick(total, 1)
    alpha0 = norm0 / cross0

    def moments(i, carry):
        norm, mixed, cross = carry
        for block in range(blocks):
            here = pl.ds(block * SUB, SUB)
            ahead = image[i + 1, chunk(block), :]
            left = field[i + 1, chunk(block), :] - alpha0 * ahead
            norm = norm + fold(left * left)
            mixed = mixed + fold(left * ahead)
            cross = cross + fold(left * (ahead - alpha0 * second[i, here, :]))
        return norm, mixed, cross

    sums = lax.fori_loop(0, depth, moments, (nothing, nothing, nothing))
    start_grp, finish_grp = across_grp(1)
    start_grp(message(sums))
    start_dev, finish_dev = across_dev(1)
    start_dev(finish_grp())
    total = finish_dev()
    norm1 = pick(total, 0)
    mixed1 = pick(total, 1)
    cross1 = pick(total, 2)
    ratio = norm1 / norm0
    alpha1 = norm1 / (cross1 + ratio * (2.0 * mixed1 + ratio * cross0))

    def finish(i, carry):
        for block in range(blocks):
            here = pl.ds(block * SUB, SUB)
            begin = field[i + 1, chunk(block), :]
            ahead = image[i + 1, chunk(block), :]
            left = begin - alpha0 * ahead
            pres_out[i, here, :] = alpha0 * begin + alpha1 * (left + ratio * begin)
            res_out[i, here, :] = left - alpha1 * (
                (ahead - alpha0 * second[i, here, :]) + ratio * ahead
            )
        return carry

    lax.fori_loop(0, depth, finish, 0)


def on_device(sizes, fraction, courant, divergence, densities, band_tiles):
    depth, rows, width = fraction.shape
    groups, devs = sizes
    padded = pltpu.VMEM((depth + 2, rows + 2 * SUB, width), jnp.float32)
    plain = pltpu.VMEM((depth, rows, width), jnp.float32)
    shape = jax.ShapeDtypeStruct((depth, rows, width), jnp.float32)
    return pl.pallas_call(
        functools.partial(kernel, sizes),
        out_shape=(shape, shape, shape),
        in_specs=[pl.BlockSpec(memory_space=pl.ANY)] * 3
        + [pl.BlockSpec(memory_space=pltpu.SMEM)] * 2,
        out_specs=[pl.BlockSpec(memory_space=pltpu.VMEM)] * 3,
        scratch_shapes=[
            padded,
            plain,
            padded,
            padded,
            plain,
            pltpu.VMEM((depth + 1, rows, width), jnp.float32),
            pltpu.VMEM((depth, rows + SUB, width), jnp.float32),
            plain,
            pltpu.VMEM((depth, rows, LANES), jnp.float32),
            pltpu.VMEM((SUB, width), jnp.float32),
            pltpu.VMEM((3, 2, depth, width), jnp.float32),
            pltpu.VMEM((3, 2, depth, width), jnp.float32),
            pltpu.VMEM((2, groups, 1, LANES), jnp.float32),
            pltpu.VMEM((2, devs, 1, LANES), jnp.float32),
            pltpu.SemaphoreType.DMA((3,)),
            pltpu.SemaphoreType.DMA((3, 2)),
            pltpu.SemaphoreType.DMA((3, 2)),
            pltpu.SemaphoreType.DMA((3, 2)),
            pltpu.SemaphoreType.DMA((3, 2)),
            pltpu.SemaphoreType.DMA((2, groups)),
            pltpu.SemaphoreType.DMA((2, groups)),
            pltpu.SemaphoreType.DMA((2, devs)),
            pltpu.SemaphoreType.DMA((2, devs)),
        ],
        compiler_params=pltpu.CompilerParams(
            collective_id=0, has_side_effects=True, vmem_limit_bytes=60 * 1024 * 1024
        ),
    )(fraction, courant, divergence, densities, band_tiles.reshape(-1))


def solution(mesh):
    sizes = (mesh.shape["grp"], mesh.shape["dev"])
    placed = P("grp", "dev", None)
    return jax.shard_map(
        functools.partial(on_device, sizes),
        mesh=mesh,
        in_specs=(placed, placed, placed, P(), placed),
        out_specs=(placed, placed, placed),
        check_vma=False,
    )
```

```python
import functools

import jax
import jax.numpy as jnp
from jax import lax
from jax.experimental import pallas as pl
from jax.experimental.pallas import tpu as pltpu
from jax.sharding import PartitionSpec as P

TILE = 16
SUB = 8
LANES = 128
MIB = 1024 * 1024
MESH = pl.DeviceIdType.MESH


def fold(value):
    total = value[:, 0:LANES]
    for start in range(LANES, value.shape[1], LANES):
        total = total + value[:, start : start + LANES]
    return total


def kernel(
    sizes,
    frac_in,
    cour_in,
    div_in,
    dens,
    band,
    moved,
    field,
    image,
    second,
    factors,
    frac,
    cour,
    beta0,
    beta1,
    beta2,
    beta_last,
    beta_top,
    mask,
    plane_recv,
    row_send,
    row_recv,
    sum_grp,
    sum_dev,
    load_sem,
    plane_send_sem,
    plane_recv_sem,
    row_send_sem,
    row_recv_sem,
    grp_send_sem,
    grp_recv_sem,
    dev_send_sem,
    dev_recv_sem,
):
    groups, devs = sizes
    depth, rows, width = frac_in.shape
    blocks = rows // SUB
    g = lax.axis_index("grp")
    d = lax.axis_index("dev")

    loads = []
    for slot, (source, target) in enumerate(
        ((frac_in, frac), (div_in, field), (cour_in, cour))
    ):
        copy = pltpu.make_async_copy(source, target, load_sem.at[slot])
        copy.start()
        loads.append(copy)

    barrier = pltpu.get_barrier_semaphore()
    for step in range(1, groups):
        pl.semaphore_signal(
            barrier, inc=1, device_id={"grp": lax.rem(g + step, groups)}, device_id_type=MESH
        )
    for step in range(1, devs):
        pl.semaphore_signal(
            barrier, inc=1, device_id={"dev": lax.rem(d + step, devs)}, device_id_type=MESH
        )

    fields = (frac, field, image)
    edges = ((g > 0, g == 0), (g < groups - 1, g == groups - 1))
    row_edges = ((d > 0, d == 0), (d < devs - 1, d == devs - 1))

    for side in range(2):

        @pl.when(edges[side][1])
        def _():
            for which in range(3):
                plane_recv[which, side] = jnp.zeros((rows, width), jnp.float32)

        @pl.when(row_edges[side][1])
        def _():
            for which in range(3):
                row_recv[which, side] = jnp.zeros((depth, width), jnp.float32)

    across = rows // TILE
    along = width // TILE
    ids = (
        lax.broadcasted_iota(jnp.int32, (SUB, width), 1) // TILE
        + lax.broadcasted_iota(jnp.int32, (SUB, width), 0) * along
    )

    def listed(entry, seen):
        return jnp.where(ids == band[entry], 1.0, seen)

    mask[...] = lax.fori_loop(
        0, across * along, listed, jnp.zeros((SUB, width), jnp.float32)
    )

    pl.semaphore_wait(barrier, groups + devs - 2)

    def plane_copy(which, side):
        plane = 0 if side == 0 else depth - 1
        source = (frac_in, div_in, image)[which]
        other = lax.rem(g + (groups - 1 if side == 0 else 1), groups)
        return pltpu.make_async_remote_copy(
            src_ref=source.at[plane],
            dst_ref=plane_recv.at[which, 1 - side],
            send_sem=plane_send_sem.at[which, side],
            recv_sem=plane_recv_sem.at[which, 1 - side],
            device_id={"grp": other},
            device_id_type=MESH,
        )

    def row_copy(which, side):
        other = lax.rem(d + (devs - 1 if side == 0 else 1), devs)
        return pltpu.make_async_remote_copy(
            src_ref=row_send.at[which, side],
            dst_ref=row_recv.at[which, 1 - side],
            send_sem=row_send_sem.at[which, side],
            recv_sem=row_recv_sem.at[which, 1 - side],
            device_id={"dev": other},
            device_id_type=MESH,
        )

    def send_planes(which):
        for side in range(2):

            @pl.when(edges[side][0])
            def _():
                plane_copy(which, side).start()

    def send_rows(which):
        source = fields[which]

        def pack(i, carry):
            row_send[which, 0, pl.ds(i, 1), :] = source[i, 0:1, :]
            row_send[which, 1, pl.ds(i, 1), :] = source[i, rows - 1 : rows, :]
            return carry

        lax.fori_loop(0, depth, pack, 0)
        for side in range(2):

            @pl.when(row_edges[side][0])
            def _():
                row_copy(which, side).start()

    def receive_rows(which):
        for side in range(2):

            @pl.when(row_edges[side][0])
            def _():
                row_copy(which, side).wait_send()
                row_copy(which, 1 - side).wait_recv()

    def receive_planes(which):
        for side in range(2):

            @pl.when(edges[side][0])
            def _():
                plane_copy(which, side).wait_send()
                plane_copy(which, 1 - side).wait_recv()

    send_planes(0)
    send_planes(1)
    loads[0].wait()
    send_rows(0)
    loads[1].wait()
    send_rows(1)

    half1 = 0.5 * dens[1]
    half_step = 0.5 * dens[0] - half1

    def half_density(value):
        return half1 + value * half_step

    edge_lane = lax.broadcasted_iota(jnp.int32, (SUB, LANES), 1)
    row = lax.broadcasted_iota(jnp.int32, (SUB, width), 0)
    first_row = row == 0
    last_row = row == SUB - 1
    tail = width - LANES

    def from_left(value, outside):
        turned = pltpu.roll(value, 1, 1)
        head = jnp.where(edge_lane == 0, outside, turned[:, :LANES])
        return jnp.concatenate([head, turned[:, LANES:]], axis=1)

    def from_right(value, outside):
        turned = pltpu.roll(value, width - 1, 1)
        end = jnp.where(edge_lane == LANES - 1, outside, turned[:, tail:])
        return jnp.concatenate([turned[:, :tail], end], axis=1)

    def here(block):
        return pl.ds(block * SUB, SUB)

    def wide(line):
        return jnp.broadcast_to(line, (SUB, width))

    def own_betas(i, before):
        turned_before = None
        for block in range(blocks):
            own = half_density(frac[i, here(block), :])
            beta2[i, here(block), :] = 1.0 / (own + from_left(own, half1))
            beta_last[i, here(block), :] = 1.0 / (own[:, tail:] + half1)
            if before:
                beta0[i, here(block), :] = 1.0 / (
                    own + half_density(frac[i - 1, here(block), :])
                )
            turned = pltpu.roll(own, 1, 0)
            south = turned
            if turned_before is not None:
                south = jnp.where(first_row, turned_before, turned)
            beta1[i, here(block), :] = 1.0 / (own + south)
            turned_before = turned

    def inner_betas(i, carry):
        own_betas(i, True)
        return carry

    own_betas(0, False)
    lax.fori_loop(1, depth, inner_betas, 0)

    receive_rows(0)
    for start in range(0, depth, SUB):
        part = pl.ds(start, SUB)
        low = half_density(row_send[0, 0, part, :]) + half_density(row_recv[0, 0, part, :])
        low = 1.0 / low
        for i in range(SUB):
            beta1[start + i, 0:1, :] = low[i : i + 1, :]
        high = half_density(row_send[0, 1, part, :]) + half_density(row_recv[0, 1, part, :])
        beta_top[part, :] = 1.0 / high

    def operator(which, i, before, after, emit):
        source = fields[which]
        turned_before = wide(row_recv[which, 0, pl.ds(i, 1), :])
        waiting = None
        for block in range(blocks):
            own = source[i, here(block), :]
            turned = pltpu.roll(own, 1, 0)
            south = jnp.where(first_row, turned_before, turned)
            flux1 = beta1[i, here(block), :] * (own - south)
            turned_flux = pltpu.roll(flux1, SUB - 1, 0)
            if waiting is not None:
                north = jnp.where(last_row, turned_flux, waiting[3])
                emit(waiting[0], waiting[1], waiting[2] - north)
            flux2 = beta2[i, here(block), :] * (own - from_left(own, 0.0))
            end = beta_last[i, here(block), :] * own[:, tail:]
            part = flux1 + (flux2 - from_right(flux2, -end))
            part = part + (
                beta0[i, here(block), :] * (own - before(block))
                + beta0[i + 1, here(block), :] * (own - after(block))
            )
            waiting = (block, own, part, turned_flux)
            turned_before = turned
        top = wide(beta_top[pl.ds(i, 1), :]) * (
            wide(row_recv[which, 1, pl.ds(i, 1), :]) - waiting[1]
        )
        north = jnp.where(last_row, top, waiting[3])
        emit(waiting[0], waiting[1], waiting[2] - north)

    def plane_of(which, i):
        source = fields[which]
        return lambda block: source[i, here(block), :]

    def halo_of(which, side):
        return lambda block: plane_recv[which, side, here(block), :]

    nothing = jnp.zeros((SUB, LANES), jnp.float32)

    def first_image(i, before, after, carry):
        sums = list(carry)

        def emit(block, own, result):
            image[i, here(block), :] = result
            sums[0] = sums[0] + fold(own * own)
            sums[1] = sums[1] + fold(own * result)

        operator(1, i, before, after, emit)
        return tuple(sums)

    def first_inner(i, carry):
        return first_image(i, plane_of(1, i - 1), plane_of(1, i + 1), carry)

    receive_rows(1)
    sums = lax.fori_loop(1, depth - 1, first_inner, (nothing, nothing))

    receive_planes(0)
    for block in range(blocks):
        low = half_density(frac[0, here(block), :])
        low = low + half_density(plane_recv[0, 0, here(block), :])
        beta0[0, here(block), :] = 1.0 / low
        high = half_density(frac[depth - 1, here(block), :])
        high = high + half_density(plane_recv[0, 1, here(block), :])
        beta0[depth, here(block), :] = 1.0 / high
    receive_planes(1)
    sums = first_image(0, halo_of(1, 0), plane_of(1, 1), sums)
    sums = first_image(depth - 1, plane_of(1, depth - 2), halo_of(1, 1), sums)

    unit = lax.broadcasted_iota(jnp.int32, (1, LANES), 1)

    def message(parts):
        value = jnp.zeros((1, LANES), jnp.float32)
        for place, part in enumerate(parts):
            value = jnp.where(unit == place, jnp.sum(part), value)
        return value

    def stage(phase, axis, buffer, send_sem, recv_sem, index, count):
        def copy(step):
            return pltpu.make_async_remote_copy(
                src_ref=buffer.at[phase, index],
                dst_ref=buffer.at[phase, index],
                send_sem=send_sem.at[phase, step],
                recv_sem=recv_sem.at[phase, step],
                device_id={axis: lax.rem(index + step, count)},
                device_id_type=MESH,
            )

        def start(value):
            buffer[phase, pl.ds(index, 1)] = value.reshape(1, 1, LANES)
            for step in range(1, count):
                copy(step).start()

        def finish():
            for step in range(1, count):
                copy(step).wait()
            total = buffer[phase, 0]
            for other in range(1, count):
                total = total + buffer[phase, other]
            return total

        return start, finish

    def across_grp(phase):
        return stage(phase, "grp", sum_grp, grp_send_sem, grp_recv_sem, g, groups)

    def across_dev(phase):
        return stage(phase, "dev", sum_dev, dev_send_sem, dev_recv_sem, d, devs)

    def pick(total, place):
        return jnp.sum(jnp.where(unit == place, total, 0.0), axis=1, keepdims=True)

    start_grp, finish_grp = across_grp(0)
    start_grp(message(sums))
    send_planes(2)
    send_rows(2)

    loads[2].wait()

    def advect(i, carry):
        for block in range(blocks):
            own = frac[i, here(block), :]
            speed = cour[i, here(block), :]
            head = jnp.where(edge_lane == 0, 0.0, speed[:, :LANES])
            speed = jnp.concatenate([head, speed[:, LANES:]], axis=1)
            left = from_left(own, 0.0)
            behind = own - left
            ahead = from_right(behind, -own[:, tail:])
            slope = jnp.maximum(0.0, jnp.minimum(ahead, behind)) + jnp.minimum(
                0.0, jnp.maximum(ahead, behind)
            )
            forward = speed > 0
            upwind = jnp.where(forward, left, own)
            tilt = jnp.where(forward, pltpu.roll(slope, 1, 1), -slope)
            flux = speed * (upwind + (0.5 - 0.5 * jnp.abs(speed)) * tilt)
            after = jnp.clip(own - (pltpu.roll(flux, width - 1, 1) - flux), 0.0, 1.0)
            flag = mask[pl.ds(block * SUB // TILE, 1), :]
            moved[i, here(block), :] = jnp.where(flag > 0.5, after, own)
        return carry

    half_way = depth // 2
    lax.fori_loop(0, half_way, advect, 0)
    start_dev, finish_dev = across_dev(0)
    start_dev(finish_grp())

    def second_image(i, before, after):
        def emit(block, own, result):
            second[i, here(block), :] = result

        operator(2, i, before, after, emit)

    def second_inner(i, carry):
        second_image(i, plane_of(2, i - 1), plane_of(2, i + 1))
        return carry

    receive_rows(2)
    lax.fori_loop(1, depth - 1, second_inner, 0)
    receive_planes(2)
    second_image(0, halo_of(2, 0), plane_of(2, 1))
    second_image(depth - 1, plane_of(2, depth - 2), halo_of(2, 1))

    total = finish_dev()
    norm0 = pick(total, 0)
    cross0 = pick(total, 1)
    alpha0 = norm0 / cross0

    def moments(i, carry):
        norm, mixed, cross = carry
        for block in range(blocks):
            ahead = image[i, here(block), :]
            left = field[i, here(block), :] - alpha0 * ahead
            norm = norm + fold(left * left)
            mixed = mixed + fold(left * ahead)
            cross = cross + fold(left * (ahead - alpha0 * second[i, here(block), :]))
        return norm, mixed, cross

    sums = lax.fori_loop(0, depth, moments, (nothing, nothing, nothing))
    start_grp, finish_grp = across_grp(1)
    start_grp(message(sums))
    three_quarters = half_way + (depth - half_way) // 2
    lax.fori_loop(half_way, three_quarters, advect, 0)
    start_dev, finish_dev = across_dev(1)
    start_dev(finish_grp())
    lax.fori_loop(three_quarters, depth, advect, 0)
    total = finish_dev()
    norm1 = pick(total, 0)
    mixed1 = pick(total, 1)
    cross1 = pick(total, 2)
    ratio = norm1 / norm0
    alpha1 = norm1 / (cross1 + ratio * (2.0 * mixed1 + ratio * cross0))
    factors[0:1, :] = jnp.broadcast_to(alpha0 + (alpha1 + alpha1 * ratio), (1, width))
    factors[1:2, :] = jnp.broadcast_to(alpha0 * alpha1, (1, width))


def closing(
    moved, field, image, second, factors, frac_out, pres_out, res_out, pres, res, sem
):
    depth, rows, width = moved.shape
    parts = 4
    size = depth // parts
    copies = [pltpu.make_async_copy(moved, frac_out, sem.at[0, parts])]
    copies[0].start()
    one = jnp.broadcast_to(factors[0:1, :], (SUB, width))
    two = jnp.broadcast_to(factors[1:2, :], (SUB, width))

    def finish(i, carry):
        for block in range(rows // SUB):
            here = pl.ds(block * SUB, SUB)
            begin = field[i, here, :]
            ahead = image[i, here, :]
            pres[i, here, :] = one * begin - two * ahead
            res[i, here, :] = begin - one * ahead + two * second[i, here, :]
        return carry

    for part in range(parts):
        lax.fori_loop(part * size, (part + 1) * size, finish, 0)
        planes = pl.ds(part * size, size)
        for place, (source, target) in enumerate(((pres, pres_out), (res, res_out))):
            copy = pltpu.make_async_copy(
                source.at[planes], target.at[planes], sem.at[place, part]
            )
            copy.start()
            copies.append(copy)
    for copy in copies:
        copy.wait()


def on_device(sizes, fraction, courant, divergence, densities, band_tiles):
    depth, rows, width = fraction.shape
    groups, devs = sizes
    block = (depth, rows, width)
    plain = pltpu.VMEM(block, jnp.float32)
    inside = pl.BlockSpec(memory_space=pltpu.VMEM)
    outside = pl.BlockSpec(memory_space=pltpu.HBM)
    held = pl.pallas_call(
        functools.partial(kernel, sizes),
        out_shape=(plain, plain, plain, plain, pltpu.VMEM((SUB, width), jnp.float32)),
        in_specs=[outside] * 3 + [pl.BlockSpec(memory_space=pltpu.SMEM)] * 2,
        out_specs=[inside] * 5,
        scratch_shapes=[
            plain,
            plain,
            pltpu.VMEM((depth + 1, rows, width), jnp.float32),
            plain,
            plain,
            pltpu.VMEM((depth, rows, LANES), jnp.float32),
            pltpu.VMEM((depth, width), jnp.float32),
            pltpu.VMEM((SUB, width), jnp.float32),
            pltpu.VMEM((3, 2, rows, width), jnp.float32),
            pltpu.VMEM((3, 2, depth, width), jnp.float32),
            pltpu.VMEM((3, 2, depth, width), jnp.float32),
            pltpu.VMEM((2, groups, 1, LANES), jnp.float32),
            pltpu.VMEM((2, devs, 1, LANES), jnp.float32),
            pltpu.SemaphoreType.DMA((3,)),
            pltpu.SemaphoreType.DMA((3, 2)),
            pltpu.SemaphoreType.DMA((3, 2)),
            pltpu.SemaphoreType.DMA((3, 2)),
            pltpu.SemaphoreType.DMA((3, 2)),
            pltpu.SemaphoreType.DMA((2, groups)),
            pltpu.SemaphoreType.DMA((2, groups)),
            pltpu.SemaphoreType.DMA((2, devs)),
            pltpu.SemaphoreType.DMA((2, devs)),
        ],
        compiler_params=pltpu.CompilerParams(
            collective_id=0, has_side_effects=True, vmem_limit_bytes=32 * MIB
        ),
        name="advance",
    )(fraction, courant, divergence, densities, band_tiles.reshape(-1))
    shape = jax.ShapeDtypeStruct(block, jnp.float32)
    return pl.pallas_call(
        closing,
        out_shape=(shape, shape, shape),
        in_specs=[inside] * 5,
        out_specs=[outside] * 3,
        scratch_shapes=[plain, plain, pltpu.SemaphoreType.DMA((2, 5))],
        compiler_params=pltpu.CompilerParams(vmem_limit_bytes=16 * MIB),
        name="closing",
    )(*held)


def solution(mesh):
    sizes = (mesh.shape["grp"], mesh.shape["dev"])
    placed = P("grp", "dev", None)
    return jax.shard_map(
        functools.partial(on_device, sizes),
        mesh=mesh,
        in_specs=(placed, placed, placed, P(), placed),
        out_specs=(placed, placed, placed),
        check_vma=False,
    )
```

```python
import functools

import jax
import jax.numpy as jnp
from jax import lax
from jax.experimental import pallas as pl
from jax.experimental.pallas import tpu as pltpu
from jax.sharding import PartitionSpec as P

TILE = 16
SUB = 8
LANES = 128
MIB = 1024 * 1024
MESH = pl.DeviceIdType.MESH


def fold(value):
    total = value[:, 0:LANES]
    for start in range(LANES, value.shape[1], LANES):
        total = total + value[:, start : start + LANES]
    return total


def kernel(
    sizes,
    frac_in,
    cour_in,
    div_in,
    dens,
    band,
    moved,
    field,
    image,
    second,
    factors,
    frac,
    cour,
    beta0,
    beta1,
    beta2,
    beta_last,
    beta_top,
    mask,
    plane_recv,
    row_send,
    row_recv,
    sum_grp,
    sum_dev,
    load_sem,
    plane_send_sem,
    plane_recv_sem,
    row_send_sem,
    row_recv_sem,
    grp_send_sem,
    grp_recv_sem,
    dev_send_sem,
    dev_recv_sem,
):
    groups, devs = sizes
    depth, rows, width = frac_in.shape
    blocks = rows // SUB
    g = lax.axis_index("grp")
    d = lax.axis_index("dev")

    loads = []
    for slot, (source, target) in enumerate(
        ((frac_in, frac), (div_in, field), (cour_in, cour))
    ):
        copy = pltpu.make_async_copy(source, target, load_sem.at[slot])
        copy.start()
        loads.append(copy)

    barrier = pltpu.get_barrier_semaphore()
    for step in range(1, groups):
        pl.semaphore_signal(
            barrier, inc=1, device_id={"grp": lax.rem(g + step, groups)}, device_id_type=MESH
        )
    for step in range(1, devs):
        pl.semaphore_signal(
            barrier, inc=1, device_id={"dev": lax.rem(d + step, devs)}, device_id_type=MESH
        )

    fields = (frac, field, image)
    edges = ((g > 0, g == 0), (g < groups - 1, g == groups - 1))
    row_edges = ((d > 0, d == 0), (d < devs - 1, d == devs - 1))

    for side in range(2):

        @pl.when(edges[side][1])
        def _():
            for which in range(3):
                plane_recv[which, side] = jnp.zeros((rows, width), jnp.float32)

        @pl.when(row_edges[side][1])
        def _():
            for which in range(3):
                row_recv[which, side] = jnp.zeros((depth, width), jnp.float32)

    across = rows // TILE
    along = width // TILE
    ids = (
        lax.broadcasted_iota(jnp.int32, (SUB, width), 1) // TILE
        + lax.broadcasted_iota(jnp.int32, (SUB, width), 0) * along
    )

    def listed(entry, seen):
        return jnp.where(ids == band[entry], 1.0, seen)

    mask[...] = lax.fori_loop(
        0, across * along, listed, jnp.zeros((SUB, width), jnp.float32)
    )

    pl.semaphore_wait(barrier, groups + devs - 2)

    def plane_copy(which, side):
        plane = 0 if side == 0 else depth - 1
        source = (frac_in, div_in, image)[which]
        other = lax.rem(g + (groups - 1 if side == 0 else 1), groups)
        return pltpu.make_async_remote_copy(
            src_ref=source.at[plane],
            dst_ref=plane_recv.at[which, 1 - side],
            send_sem=plane_send_sem.at[which, side],
            recv_sem=plane_recv_sem.at[which, 1 - side],
            device_id={"grp": other},
            device_id_type=MESH,
        )

    def row_copy(which, side):
        other = lax.rem(d + (devs - 1 if side == 0 else 1), devs)
        return pltpu.make_async_remote_copy(
            src_ref=row_send.at[which, side],
            dst_ref=row_recv.at[which, 1 - side],
            send_sem=row_send_sem.at[which, side],
            recv_sem=row_recv_sem.at[which, 1 - side],
            device_id={"dev": other},
            device_id_type=MESH,
        )

    def send_planes(which):
        for side in range(2):

            @pl.when(edges[side][0])
            def _():
                plane_copy(which, side).start()

    def send_rows(which):
        source = fields[which]

        def pack(i, carry):
            row_send[which, 0, pl.ds(i, 1), :] = source[i, 0:1, :]
            row_send[which, 1, pl.ds(i, 1), :] = source[i, rows - 1 : rows, :]
            return carry

        lax.fori_loop(0, depth, pack, 0)
        for side in range(2):

            @pl.when(row_edges[side][0])
            def _():
                row_copy(which, side).start()

    def receive_rows(which):
        for side in range(2):

            @pl.when(row_edges[side][0])
            def _():
                row_copy(which, side).wait_send()
                row_copy(which, 1 - side).wait_recv()

    def receive_planes(which):
        for side in range(2):

            @pl.when(edges[side][0])
            def _():
                plane_copy(which, side).wait_send()
                plane_copy(which, 1 - side).wait_recv()

    send_planes(0)
    send_planes(1)
    loads[0].wait()
    send_rows(0)
    loads[1].wait()
    send_rows(1)

    half1 = 0.5 * dens[1]
    half_step = 0.5 * dens[0] - half1

    def half_density(value):
        return half1 + value * half_step

    edge_lane = lax.broadcasted_iota(jnp.int32, (SUB, LANES), 1)
    row = lax.broadcasted_iota(jnp.int32, (SUB, width), 0)
    first_row = row == 0
    last_row = row == SUB - 1
    tail = width - LANES

    def from_left(value, outside):
        turned = pltpu.roll(value, 1, 1)
        head = jnp.where(edge_lane == 0, outside, turned[:, :LANES])
        return jnp.concatenate([head, turned[:, LANES:]], axis=1)

    def from_right(value, outside):
        turned = pltpu.roll(value, width - 1, 1)
        end = jnp.where(edge_lane == LANES - 1, outside, turned[:, tail:])
        return jnp.concatenate([turned[:, :tail], end], axis=1)

    def here(block):
        return pl.ds(block * SUB, SUB)

    def wide(line):
        return jnp.broadcast_to(line, (SUB, width))

    def own_betas(i, before):
        turned_before = None
        for block in range(blocks):
            own = half_density(frac[i, here(block), :])
            beta2[i, here(block), :] = 1.0 / (own + from_left(own, half1))
            beta_last[i, here(block), :] = 1.0 / (own[:, tail:] + half1)
            if before:
                beta0[i, here(block), :] = 1.0 / (
                    own + half_density(frac[i - 1, here(block), :])
                )
            turned = pltpu.roll(own, 1, 0)
            south = turned
            if turned_before is not None:
                south = jnp.where(first_row, turned_before, turned)
            beta1[i, here(block), :] = 1.0 / (own + south)
            turned_before = turned

    def inner_betas(i, carry):
        own_betas(i, True)
        return carry

    own_betas(0, False)
    lax.fori_loop(1, depth, inner_betas, 0)

    receive_rows(0)
    for start in range(0, depth, SUB):
        part = pl.ds(start, SUB)
        low = half_density(row_send[0, 0, part, :]) + half_density(row_recv[0, 0, part, :])
        low = 1.0 / low
        for i in range(SUB):
            beta1[start + i, 0:1, :] = low[i : i + 1, :]
        high = half_density(row_send[0, 1, part, :]) + half_density(row_recv[0, 1, part, :])
        beta_top[part, :] = 1.0 / high

    def operator(which, i, before, after, emit):
        source = fields[which]
        turned_before = wide(row_recv[which, 0, pl.ds(i, 1), :])
        waiting = None
        for block in range(blocks):
            own = source[i, here(block), :]
            turned = pltpu.roll(own, 1, 0)
            south = jnp.where(first_row, turned_before, turned)
            flux1 = beta1[i, here(block), :] * (own - south)
            turned_flux = pltpu.roll(flux1, SUB - 1, 0)
            if waiting is not None:
                north = jnp.where(last_row, turned_flux, waiting[3])
                emit(waiting[0], waiting[1], waiting[2] - north)
            flux2 = beta2[i, here(block), :] * (own - from_left(own, 0.0))
            end = beta_last[i, here(block), :] * own[:, tail:]
            part = flux1 + (flux2 - from_right(flux2, -end))
            part = part + (
                beta0[i, here(block), :] * (own - before(block))
                + beta0[i + 1, here(block), :] * (own - after(block))
            )
            waiting = (block, own, part, turned_flux)
            turned_before = turned
        top = wide(beta_top[pl.ds(i, 1), :]) * (
            wide(row_recv[which, 1, pl.ds(i, 1), :]) - waiting[1]
        )
        north = jnp.where(last_row, top, waiting[3])
        emit(waiting[0], waiting[1], waiting[2] - north)

    def plane_of(which, i):
        source = fields[which]
        return lambda block: source[i, here(block), :]

    def halo_of(which, side):
        return lambda block: plane_recv[which, side, here(block), :]

    nothing = jnp.zeros((SUB, LANES), jnp.float32)

    def first_image(i, before, after, carry):
        sums = list(carry)

        def emit(block, own, result):
            image[i, here(block), :] = result
            sums[0] = sums[0] + fold(own * own)
            sums[1] = sums[1] + fold(own * result)

        operator(1, i, before, after, emit)
        return tuple(sums)

    def first_inner(i, carry):
        return first_image(i, plane_of(1, i - 1), plane_of(1, i + 1), carry)

    receive_rows(1)
    sums = lax.fori_loop(1, depth - 1, first_inner, (nothing, nothing))

    receive_planes(0)
    for block in range(blocks):
        low = half_density(frac[0, here(block), :])
        low = low + half_density(plane_recv[0, 0, here(block), :])
        beta0[0, here(block), :] = 1.0 / low
        high = half_density(frac[depth - 1, here(block), :])
        high = high + half_density(plane_recv[0, 1, here(block), :])
        beta0[depth, here(block), :] = 1.0 / high
    receive_planes(1)
    sums = first_image(0, halo_of(1, 0), plane_of(1, 1), sums)
    sums = first_image(depth - 1, plane_of(1, depth - 2), halo_of(1, 1), sums)

    unit = lax.broadcasted_iota(jnp.int32, (1, LANES), 1)

    def message(parts):
        value = jnp.zeros((1, LANES), jnp.float32)
        for place, part in enumerate(parts):
            value = jnp.where(unit == place, jnp.sum(part), value)
        return value

    def stage(phase, axis, buffer, send_sem, recv_sem, index, count):
        def copy(step):
            return pltpu.make_async_remote_copy(
                src_ref=buffer.at[phase, index],
                dst_ref=buffer.at[phase, index],
                send_sem=send_sem.at[phase, step],
                recv_sem=recv_sem.at[phase, step],
                device_id={axis: lax.rem(index + step, count)},
                device_id_type=MESH,
            )

        def start(value):
            buffer[phase, pl.ds(index, 1)] = value.reshape(1, 1, LANES)
            for step in range(1, count):
                copy(step).start()

        def finish():
            for step in range(1, count):
                copy(step).wait()
            total = buffer[phase, 0]
            for other in range(1, count):
                total = total + buffer[phase, other]
            return total

        return start, finish

    def across_grp(phase):
        return stage(phase, "grp", sum_grp, grp_send_sem, grp_recv_sem, g, groups)

    def across_dev(phase):
        return stage(phase, "dev", sum_dev, dev_send_sem, dev_recv_sem, d, devs)

    def pick(total, place):
        return jnp.sum(jnp.where(unit == place, total, 0.0), axis=1, keepdims=True)

    start_grp, finish_grp = across_grp(0)
    start_grp(message(sums))
    send_planes(2)
    send_rows(2)

    loads[2].wait()

    def advect(i, carry):
        for block in range(blocks):
            own = frac[i, here(block), :]
            speed = cour[i, here(block), :]
            head = jnp.where(edge_lane == 0, 0.0, speed[:, :LANES])
            speed = jnp.concatenate([head, speed[:, LANES:]], axis=1)
            left = from_left(own, 0.0)
            behind = own - left
            ahead = from_right(behind, -own[:, tail:])
            slope = jnp.maximum(0.0, jnp.minimum(ahead, behind)) + jnp.minimum(
                0.0, jnp.maximum(ahead, behind)
            )
            forward = speed > 0
            upwind = jnp.where(forward, left, own)
            tilt = jnp.where(forward, pltpu.roll(slope, 1, 1), -slope)
            flux = speed * (upwind + (0.5 - 0.5 * jnp.abs(speed)) * tilt)
            after = jnp.clip(own - (pltpu.roll(flux, width - 1, 1) - flux), 0.0, 1.0)
            flag = mask[pl.ds(block * SUB // TILE, 1), :]
            moved[i, here(block), :] = jnp.where(flag > 0.5, after, own)
        return carry

    half_way = depth // 2
    lax.fori_loop(0, half_way, advect, 0)
    start_dev, finish_dev = across_dev(0)
    start_dev(finish_grp())

    def second_image(i, before, after):
        def emit(block, own, result):
            second[i, here(block), :] = result

        operator(2, i, before, after, emit)

    def second_inner(i, carry):
        second_image(i, plane_of(2, i - 1), plane_of(2, i + 1))
        return carry

    receive_rows(2)
    lax.fori_loop(1, depth - 1, second_inner, 0)
    receive_planes(2)
    second_image(0, halo_of(2, 0), plane_of(2, 1))
    second_image(depth - 1, plane_of(2, depth - 2), halo_of(2, 1))

    total = finish_dev()
    norm0 = pick(total, 0)
    cross0 = pick(total, 1)
    alpha0 = norm0 / cross0

    def moments(i, carry):
        norm, mixed, cross = carry
        for block in range(blocks):
            ahead = image[i, here(block), :]
            left = field[i, here(block), :] - alpha0 * ahead
            norm = norm + fold(left * left)
            mixed = mixed + fold(left * ahead)
            cross = cross + fold(left * (ahead - alpha0 * second[i, here(block), :]))
        return norm, mixed, cross

    sums = lax.fori_loop(0, depth, moments, (nothing, nothing, nothing))
    start_grp, finish_grp = across_grp(1)
    start_grp(message(sums))
    three_quarters = half_way + (depth - half_way) // 2
    lax.fori_loop(half_way, three_quarters, advect, 0)
    start_dev, finish_dev = across_dev(1)
    start_dev(finish_grp())
    lax.fori_loop(three_quarters, depth, advect, 0)
    total = finish_dev()
    norm1 = pick(total, 0)
    mixed1 = pick(total, 1)
    cross1 = pick(total, 2)
    ratio = norm1 / norm0
    alpha1 = norm1 / (cross1 + ratio * (2.0 * mixed1 + ratio * cross0))
    factors[0:1, :] = jnp.broadcast_to(alpha0 + (alpha1 + alpha1 * ratio), (1, width))
    factors[1:2, :] = jnp.broadcast_to(alpha0 * alpha1, (1, width))


def closing(
    moved, field, image, second, factors, frac_out, pres_out, res_out, pres, res, sem
):
    depth, rows, width = moved.shape
    parts = 4
    size = depth // parts
    copies = [pltpu.make_async_copy(moved, frac_out, sem.at[0, parts])]
    copies[0].start()
    one = jnp.broadcast_to(factors[0:1, :], (SUB, width))
    two = jnp.broadcast_to(factors[1:2, :], (SUB, width))

    def finish(i, carry):
        for block in range(rows // SUB):
            here = pl.ds(block * SUB, SUB)
            begin = field[i, here, :]
            ahead = image[i, here, :]
            pres[i, here, :] = one * begin - two * ahead
            res[i, here, :] = begin - one * ahead + two * second[i, here, :]
        return carry

    for part in range(parts):
        lax.fori_loop(part * size, (part + 1) * size, finish, 0)
        planes = pl.ds(part * size, size)
        for place, (source, target) in enumerate(((pres, pres_out), (res, res_out))):
            copy = pltpu.make_async_copy(
                source.at[planes], target.at[planes], sem.at[place, part]
            )
            copy.start()
            copies.append(copy)
    for copy in copies:
        copy.wait()


def on_device(sizes, fraction, courant, divergence, densities, band_tiles):
    depth, rows, width = fraction.shape
    groups, devs = sizes
    block = (depth, rows, width)
    plain = pltpu.VMEM(block, jnp.float32)
    inside = pl.BlockSpec(memory_space=pltpu.VMEM)
    outside = pl.BlockSpec(memory_space=pltpu.HBM)
    kept = [pltpu.with_memory_space_constraint(x, pltpu.HBM) for x in (fraction, courant, divergence)]
    held = pl.pallas_call(
        functools.partial(kernel, sizes),
        out_shape=(plain, plain, plain, plain, pltpu.VMEM((SUB, width), jnp.float32)),
        in_specs=[outside] * 3 + [pl.BlockSpec(memory_space=pltpu.SMEM)] * 2,
        out_specs=[inside] * 5,
        scratch_shapes=[
            plain,
            plain,
            pltpu.VMEM((depth + 1, rows, width), jnp.float32),
            plain,
            plain,
            pltpu.VMEM((depth, rows, LANES), jnp.float32),
            pltpu.VMEM((depth, width), jnp.float32),
            pltpu.VMEM((SUB, width), jnp.float32),
            pltpu.VMEM((3, 2, rows, width), jnp.float32),
            pltpu.VMEM((3, 2, depth, width), jnp.float32),
            pltpu.VMEM((3, 2, depth, width), jnp.float32),
            pltpu.VMEM((2, groups, 1, LANES), jnp.float32),
            pltpu.VMEM((2, devs, 1, LANES), jnp.float32),
            pltpu.SemaphoreType.DMA((3,)),
            pltpu.SemaphoreType.DMA((3, 2)),
            pltpu.SemaphoreType.DMA((3, 2)),
            pltpu.SemaphoreType.DMA((3, 2)),
            pltpu.SemaphoreType.DMA((3, 2)),
            pltpu.SemaphoreType.DMA((2, groups)),
            pltpu.SemaphoreType.DMA((2, groups)),
            pltpu.SemaphoreType.DMA((2, devs)),
            pltpu.SemaphoreType.DMA((2, devs)),
        ],
        compiler_params=pltpu.CompilerParams(
            collective_id=0, has_side_effects=True, vmem_limit_bytes=55 * MIB
        ),
        name="advance",
    )(*kept, densities, band_tiles.reshape(-1))
    shape = jax.ShapeDtypeStruct(block, jnp.float32)
    return pl.pallas_call(
        closing,
        out_shape=(shape, shape, shape),
        in_specs=[inside] * 5,
        out_specs=[outside] * 3,
        scratch_shapes=[plain, plain, pltpu.SemaphoreType.DMA((2, 5))],
        compiler_params=pltpu.CompilerParams(vmem_limit_bytes=16 * MIB),
        name="closing",
    )(*held)


def solution(mesh):
    sizes = (mesh.shape["grp"], mesh.shape["dev"])
    placed = P("grp", "dev", None)
    return jax.shard_map(
        functools.partial(on_device, sizes),
        mesh=mesh,
        in_specs=(placed, placed, placed, P(), placed),
        out_specs=(placed, placed, placed),
        check_vma=False,
    )
```

```python
import functools

import jax
import jax.numpy as jnp
from jax import lax
from jax.experimental import pallas as pl
from jax.experimental.pallas import tpu as pltpu
from jax.sharding import PartitionSpec as P

TILE = 16
SUB = 8
LANES = 128
MIB = 1024 * 1024
MESH = pl.DeviceIdType.MESH


def fold(value):
    total = value[:, 0:LANES]
    for start in range(LANES, value.shape[1], LANES):
        total = total + value[:, start : start + LANES]
    return total


def kernel(
    sizes,
    frac_in,
    cour_in,
    div_in,
    dens,
    band,
    moved,
    field,
    image,
    second,
    factors,
    frac,
    cour,
    beta0,
    beta1,
    beta2,
    beta_last,
    beta_top,
    mask,
    plane_recv,
    row_send,
    row_recv,
    shared,
    load_sem,
    plane_send_sem,
    plane_recv_sem,
    row_send_sem,
    row_recv_sem,
    sum_send_sem,
    sum_recv_sem,
):
    groups, devs = sizes
    depth, rows, width = frac_in.shape
    blocks = rows // SUB
    g = lax.axis_index("grp")
    d = lax.axis_index("dev")

    loads = []
    for slot, (source, target) in enumerate(
        ((frac_in, frac), (div_in, field), (cour_in, cour))
    ):
        copy = pltpu.make_async_copy(source, target, load_sem.at[slot])
        copy.start()
        loads.append(copy)

    barrier = pltpu.get_barrier_semaphore()
    count = groups * devs
    rank = g * devs + d

    def partner(step):
        other = lax.rem(rank + step, count)
        return {"grp": other // devs, "dev": lax.rem(other, devs)}

    for step in range(1, count):
        pl.semaphore_signal(barrier, inc=1, device_id=partner(step), device_id_type=MESH)

    fields = (frac, field, image)
    edges = ((g > 0, g == 0), (g < groups - 1, g == groups - 1))
    row_edges = ((d > 0, d == 0), (d < devs - 1, d == devs - 1))

    for side in range(2):

        @pl.when(edges[side][1])
        def _():
            for which in range(3):
                plane_recv[which, side] = jnp.zeros((rows, width), jnp.float32)

        @pl.when(row_edges[side][1])
        def _():
            for which in range(3):
                row_recv[which, side] = jnp.zeros((depth, width), jnp.float32)

    across = rows // TILE
    along = width // TILE
    ids = (
        lax.broadcasted_iota(jnp.int32, (SUB, width), 1) // TILE
        + lax.broadcasted_iota(jnp.int32, (SUB, width), 0) * along
    )

    def listed(entry, seen):
        return jnp.where(ids == band[entry], 1.0, seen)

    mask[...] = lax.fori_loop(
        0, across * along, listed, jnp.zeros((SUB, width), jnp.float32)
    )

    pl.semaphore_wait(barrier, count - 1)

    def plane_copy(which, side):
        plane = 0 if side == 0 else depth - 1
        source = (frac_in, div_in, image)[which]
        other = lax.rem(g + (groups - 1 if side == 0 else 1), groups)
        return pltpu.make_async_remote_copy(
            src_ref=source.at[plane],
            dst_ref=plane_recv.at[which, 1 - side],
            send_sem=plane_send_sem.at[which, side],
            recv_sem=plane_recv_sem.at[which, 1 - side],
            device_id={"grp": other},
            device_id_type=MESH,
        )

    def row_copy(which, side):
        other = lax.rem(d + (devs - 1 if side == 0 else 1), devs)
        return pltpu.make_async_remote_copy(
            src_ref=row_send.at[which, side],
            dst_ref=row_recv.at[which, 1 - side],
            send_sem=row_send_sem.at[which, side],
            recv_sem=row_recv_sem.at[which, 1 - side],
            device_id={"dev": other},
            device_id_type=MESH,
        )

    def send_planes(which):
        for side in range(2):

            @pl.when(edges[side][0])
            def _():
                plane_copy(which, side).start()

    def send_rows(which):
        source = fields[which]

        def pack(i, carry):
            row_send[which, 0, pl.ds(i, 1), :] = source[i, 0:1, :]
            row_send[which, 1, pl.ds(i, 1), :] = source[i, rows - 1 : rows, :]
            return carry

        lax.fori_loop(0, depth, pack, 0)
        for side in range(2):

            @pl.when(row_edges[side][0])
            def _():
                row_copy(which, side).start()

    def receive_rows(which):
        for side in range(2):

            @pl.when(row_edges[side][0])
            def _():
                row_copy(which, side).wait_send()
                row_copy(which, 1 - side).wait_recv()

    def receive_planes(which):
        for side in range(2):

            @pl.when(edges[side][0])
            def _():
                plane_copy(which, side).wait_send()
                plane_copy(which, 1 - side).wait_recv()

    send_planes(0)
    send_planes(1)
    loads[0].wait()
    send_rows(0)
    loads[1].wait()
    send_rows(1)

    half1 = 0.5 * dens[1]
    half_step = 0.5 * dens[0] - half1

    def half_density(value):
        return half1 + value * half_step

    edge_lane = lax.broadcasted_iota(jnp.int32, (SUB, LANES), 1)
    row = lax.broadcasted_iota(jnp.int32, (SUB, width), 0)
    first_row = row == 0
    last_row = row == SUB - 1
    tail = width - LANES

    def from_left(value, outside):
        turned = pltpu.roll(value, 1, 1)
        head = jnp.where(edge_lane == 0, outside, turned[:, :LANES])
        return jnp.concatenate([head, turned[:, LANES:]], axis=1)

    def from_right(value, outside):
        turned = pltpu.roll(value, width - 1, 1)
        end = jnp.where(edge_lane == LANES - 1, outside, turned[:, tail:])
        return jnp.concatenate([turned[:, :tail], end], axis=1)

    def here(block):
        return pl.ds(block * SUB, SUB)

    def wide(line):
        return jnp.broadcast_to(line, (SUB, width))

    def own_betas(i, before):
        turned_before = None
        for block in range(blocks):
            own = half_density(frac[i, here(block), :])
            beta2[i, here(block), :] = 1.0 / (own + from_left(own, half1))
            beta_last[i, here(block), :] = 1.0 / (own[:, tail:] + half1)
            if before:
                beta0[i, here(block), :] = 1.0 / (
                    own + half_density(frac[i - 1, here(block), :])
                )
            turned = pltpu.roll(own, 1, 0)
            south = turned
            if turned_before is not None:
                south = jnp.where(first_row, turned_before, turned)
            beta1[i, here(block), :] = 1.0 / (own + south)
            turned_before = turned

    def inner_betas(i, carry):
        own_betas(i, True)
        return carry

    own_betas(0, False)
    lax.fori_loop(1, depth, inner_betas, 0)

    receive_rows(0)
    for start in range(0, depth, SUB):
        part = pl.ds(start, SUB)
        low = half_density(row_send[0, 0, part, :]) + half_density(row_recv[0, 0, part, :])
        low = 1.0 / low
        for i in range(SUB):
            beta1[start + i, 0:1, :] = low[i : i + 1, :]
        high = half_density(row_send[0, 1, part, :]) + half_density(row_recv[0, 1, part, :])
        beta_top[part, :] = 1.0 / high

    def operator(which, i, before, after, emit):
        source = fields[which]
        turned_before = wide(row_recv[which, 0, pl.ds(i, 1), :])
        waiting = None
        for block in range(blocks):
            own = source[i, here(block), :]
            turned = pltpu.roll(own, 1, 0)
            south = jnp.where(first_row, turned_before, turned)
            flux1 = beta1[i, here(block), :] * (own - south)
            turned_flux = pltpu.roll(flux1, SUB - 1, 0)
            if waiting is not None:
                north = jnp.where(last_row, turned_flux, waiting[3])
                emit(waiting[0], waiting[1], waiting[2] - north)
            flux2 = beta2[i, here(block), :] * (own - from_left(own, 0.0))
            end = beta_last[i, here(block), :] * own[:, tail:]
            part = flux1 + (flux2 - from_right(flux2, -end))
            part = part + (
                beta0[i, here(block), :] * (own - before(block))
                + beta0[i + 1, here(block), :] * (own - after(block))
            )
            waiting = (block, own, part, turned_flux)
            turned_before = turned
        top = wide(beta_top[pl.ds(i, 1), :]) * (
            wide(row_recv[which, 1, pl.ds(i, 1), :]) - waiting[1]
        )
        north = jnp.where(last_row, top, waiting[3])
        emit(waiting[0], waiting[1], waiting[2] - north)

    def plane_of(which, i):
        source = fields[which]
        return lambda block: source[i, here(block), :]

    def halo_of(which, side):
        return lambda block: plane_recv[which, side, here(block), :]

    nothing = jnp.zeros((SUB, LANES), jnp.float32)

    def first_image(i, before, after, carry):
        sums = list(carry)

        def emit(block, own, result):
            image[i, here(block), :] = result
            sums[0] = sums[0] + fold(own * own)
            sums[1] = sums[1] + fold(own * result)

        operator(1, i, before, after, emit)
        return tuple(sums)

    def first_inner(i, carry):
        return first_image(i, plane_of(1, i - 1), plane_of(1, i + 1), carry)

    receive_rows(1)
    sums = lax.fori_loop(1, depth - 1, first_inner, (nothing, nothing))

    receive_planes(0)
    for block in range(blocks):
        low = half_density(frac[0, here(block), :])
        low = low + half_density(plane_recv[0, 0, here(block), :])
        beta0[0, here(block), :] = 1.0 / low
        high = half_density(frac[depth - 1, here(block), :])
        high = high + half_density(plane_recv[0, 1, here(block), :])
        beta0[depth, here(block), :] = 1.0 / high
    receive_planes(1)
    sums = first_image(0, halo_of(1, 0), plane_of(1, 1), sums)
    sums = first_image(depth - 1, plane_of(1, depth - 2), halo_of(1, 1), sums)

    unit = lax.broadcasted_iota(jnp.int32, (1, LANES), 1)

    def message(parts):
        value = jnp.zeros((1, LANES), jnp.float32)
        for place, part in enumerate(parts):
            value = jnp.where(unit == place, jnp.sum(part), value)
        return value

    def all_devices(phase):
        def copy(step):
            return pltpu.make_async_remote_copy(
                src_ref=shared.at[phase, rank],
                dst_ref=shared.at[phase, rank],
                send_sem=sum_send_sem.at[phase, step],
                recv_sem=sum_recv_sem.at[phase, step],
                device_id=partner(step),
                device_id_type=MESH,
            )

        def start(value):
            shared[phase, pl.ds(rank, 1)] = value.reshape(1, 1, LANES)
            for step in range(1, count):
                copy(step).start()

        def finish():
            for step in range(1, count):
                copy(step).wait()
            return jnp.sum(shared[phase], axis=0)

        return start, finish

    def pick(total, place):
        return jnp.sum(jnp.where(unit == place, total, 0.0), axis=1, keepdims=True)

    start_sums, finish_sums = all_devices(0)
    start_sums(message(sums))
    send_planes(2)
    send_rows(2)

    loads[2].wait()

    def advect(i, carry):
        for block in range(blocks):
            own = frac[i, here(block), :]
            speed = cour[i, here(block), :]
            head = jnp.where(edge_lane == 0, 0.0, speed[:, :LANES])
            speed = jnp.concatenate([head, speed[:, LANES:]], axis=1)
            left = from_left(own, 0.0)
            behind = own - left
            ahead = from_right(behind, -own[:, tail:])
            slope = jnp.maximum(0.0, jnp.minimum(ahead, behind)) + jnp.minimum(
                0.0, jnp.maximum(ahead, behind)
            )
            forward = speed > 0
            upwind = jnp.where(forward, left, own)
            tilt = jnp.where(forward, pltpu.roll(slope, 1, 1), -slope)
            flux = speed * (upwind + (0.5 - 0.5 * jnp.abs(speed)) * tilt)
            after = jnp.clip(own - (pltpu.roll(flux, width - 1, 1) - flux), 0.0, 1.0)
            flag = mask[pl.ds(block * SUB // TILE, 1), :]
            moved[i, here(block), :] = jnp.where(flag > 0.5, after, own)
        return carry

    half_way = depth // 2
    lax.fori_loop(0, half_way, advect, 0)

    def second_image(i, before, after):
        def emit(block, own, result):
            second[i, here(block), :] = result

        operator(2, i, before, after, emit)

    def second_inner(i, carry):
        second_image(i, plane_of(2, i - 1), plane_of(2, i + 1))
        return carry

    receive_rows(2)
    lax.fori_loop(1, depth - 1, second_inner, 0)
    receive_planes(2)
    second_image(0, halo_of(2, 0), plane_of(2, 1))
    second_image(depth - 1, plane_of(2, depth - 2), halo_of(2, 1))

    total = finish_sums()
    norm0 = pick(total, 0)
    cross0 = pick(total, 1)
    alpha0 = norm0 / cross0

    def moments(i, carry):
        norm, mixed, cross = carry
        for block in range(blocks):
            ahead = image[i, here(block), :]
            left = field[i, here(block), :] - alpha0 * ahead
            norm = norm + fold(left * left)
            mixed = mixed + fold(left * ahead)
            cross = cross + fold(left * (ahead - alpha0 * second[i, here(block), :]))
        return norm, mixed, cross

    sums = lax.fori_loop(0, depth, moments, (nothing, nothing, nothing))
    start_sums, finish_sums = all_devices(1)
    start_sums(message(sums))
    lax.fori_loop(half_way, depth, advect, 0)
    total = finish_sums()
    norm1 = pick(total, 0)
    mixed1 = pick(total, 1)
    cross1 = pick(total, 2)
    ratio = norm1 / norm0
    alpha1 = norm1 / (cross1 + ratio * (2.0 * mixed1 + ratio * cross0))
    factors[0:1, :] = jnp.broadcast_to(alpha0 + (alpha1 + alpha1 * ratio), (1, width))
    factors[1:2, :] = jnp.broadcast_to(alpha0 * alpha1, (1, width))


def closing(
    moved, field, image, second, factors, frac_out, pres_out, res_out, pres, res, sem
):
    depth, rows, width = moved.shape
    parts = 4
    size = depth // parts
    copies = [pltpu.make_async_copy(moved, frac_out, sem.at[0, parts])]
    copies[0].start()
    one = jnp.broadcast_to(factors[0:1, :], (SUB, width))
    two = jnp.broadcast_to(factors[1:2, :], (SUB, width))

    def finish(i, carry):
        for block in range(rows // SUB):
            here = pl.ds(block * SUB, SUB)
            begin = field[i, here, :]
            ahead = image[i, here, :]
            pres[i, here, :] = one * begin - two * ahead
            res[i, here, :] = begin - one * ahead + two * second[i, here, :]
        return carry

    for part in range(parts):
        lax.fori_loop(part * size, (part + 1) * size, finish, 0)
        planes = pl.ds(part * size, size)
        for place, (source, target) in enumerate(((pres, pres_out), (res, res_out))):
            copy = pltpu.make_async_copy(
                source.at[planes], target.at[planes], sem.at[place, part]
            )
            copy.start()
            copies.append(copy)
    for copy in copies:
        copy.wait()


def on_device(sizes, fraction, courant, divergence, densities, band_tiles):
    depth, rows, width = fraction.shape
    groups, devs = sizes
    block = (depth, rows, width)
    plain = pltpu.VMEM(block, jnp.float32)
    inside = pl.BlockSpec(memory_space=pltpu.VMEM)
    outside = pl.BlockSpec(memory_space=pltpu.HBM)
    kept = [pltpu.with_memory_space_constraint(x, pltpu.HBM) for x in (fraction, courant, divergence)]
    held = pl.pallas_call(
        functools.partial(kernel, sizes),
        out_shape=(plain, plain, plain, plain, pltpu.VMEM((SUB, width), jnp.float32)),
        in_specs=[outside] * 3 + [pl.BlockSpec(memory_space=pltpu.SMEM)] * 2,
        out_specs=[inside] * 5,
        scratch_shapes=[
            plain,
            plain,
            pltpu.VMEM((depth + 1, rows, width), jnp.float32),
            plain,
            plain,
            pltpu.VMEM((depth, rows, LANES), jnp.float32),
            pltpu.VMEM((depth, width), jnp.float32),
            pltpu.VMEM((SUB, width), jnp.float32),
            pltpu.VMEM((3, 2, rows, width), jnp.float32),
            pltpu.VMEM((3, 2, depth, width), jnp.float32),
            pltpu.VMEM((3, 2, depth, width), jnp.float32),
            pltpu.VMEM((2, groups * devs, 1, LANES), jnp.float32),
            pltpu.SemaphoreType.DMA((3,)),
            pltpu.SemaphoreType.DMA((3, 2)),
            pltpu.SemaphoreType.DMA((3, 2)),
            pltpu.SemaphoreType.DMA((3, 2)),
            pltpu.SemaphoreType.DMA((3, 2)),
            pltpu.SemaphoreType.DMA((2, groups * devs)),
            pltpu.SemaphoreType.DMA((2, groups * devs)),
        ],
        compiler_params=pltpu.CompilerParams(
            collective_id=0, has_side_effects=True, vmem_limit_bytes=55 * MIB
        ),
        name="advance",
    )(*kept, densities, band_tiles.reshape(-1))
    shape = jax.ShapeDtypeStruct(block, jnp.float32)
    return pl.pallas_call(
        closing,
        out_shape=(shape, shape, shape),
        in_specs=[inside] * 5,
        out_specs=[outside] * 3,
        scratch_shapes=[plain, plain, pltpu.SemaphoreType.DMA((2, 5))],
        compiler_params=pltpu.CompilerParams(vmem_limit_bytes=16 * MIB),
        name="closing",
    )(*held)


def solution(mesh):
    sizes = (mesh.shape["grp"], mesh.shape["dev"])
    placed = P("grp", "dev", None)
    return jax.shard_map(
        functools.partial(on_device, sizes),
        mesh=mesh,
        in_specs=(placed, placed, placed, P(), placed),
        out_specs=(placed, placed, placed),
        check_vma=False,
    )
```
